1024 devices in a mesh: dp: 64 (over z, core), tensor: 16 (over y, x).
Axes of the slice: x: 4, y: 4, z: 32, core: 2. Of those that a mesh axis runs over, the one named last changes fastest.
Arguments:
- hidden_acts: bfloat16 [49152, 28672], P('dp', 'tensor'), may hold values from -6 to 6
- out_grads: bfloat16 [49152, 8192], P(('dp', 'tensor')), may hold values from -6 to 6
- seq_of_token: int32 [49152], P('dp'), may hold values from 0 to 1, as said below
- proj_in: bfloat16 [28672, 256], P('tensor'), may hold values from -0.046875 to 0.046875
- proj_out: bfloat16 [8192, 128], replicated, may hold values from -0.0034179688 to 0.0034179688
Outputs:
- example_grads: float32 [128, 256, 128], P('dp', 'tensor')
The draws below stay inside these ranges and needn't reach their ends.
Inputs may be any that keep to these rules, and one draw needn't show every extreme that they name: `seq_of_token`: within the tokens of one index of dp the value never falls, starts at 0, and each of the 2 sequences holds at least one token.
All inputs are finite; a program needn't handle non-finite values.
Results may differ from the reference program's by a relative error of at most 0.0003.
Values may be sent and summed in bfloat16 or wider, within the bound.
A program may use at most 32 MiB of HBM per device.

```python
import jax
import jax.numpy as jnp
from jax import lax

D = 8192
FF = 28672
K_IN = 256
K_OUT = 128
SEQ_DEV = 2
TOK_DEV = 768
TOKENS = 49152
SEQS = 128


def draw_seq_of_token(key, part):
    blocks_count = TOKENS // TOK_DEV
    keys = jax.random.split(key, blocks_count)

    def one_block(block_key):
        shuffled = jax.random.permutation(block_key, TOK_DEV - 1) + 1
        cuts = jnp.sort(shuffled[:SEQ_DEV - 1])
        positions = jnp.arange(TOK_DEV, dtype=jnp.int32)
        return jnp.sum((positions[:, None] >= cuts[None, :]).astype(jnp.int32), axis=1).astype(jnp.int32)
    return jax.vmap(one_block)(keys).reshape(-1).astype(jnp.int32)


def with_spikes(array, stream_key, source, target, parts, factor):
    def block_of(position):
        return (jnp.arange(array.shape[position]) // (array.shape[position] // parts)).reshape((-1,) + (1,) * (array.ndim - 1 - position))

    first = jax.random.permutation(stream_key, parts)[block_of(target)]
    second = (block_of(target) + parts // 2) % parts
    return jnp.where((block_of(source) == first) | (block_of(source) == second), factor * array, array)


def level_of(own_key, dims, cuts, smallest, top_value):
    factor_of, own = 1.0, jax.random.fold_in(own_key, 6)
    for axis_at, parts in cuts:
        draws = jnp.exp(jax.random.uniform(jax.random.fold_in(own, axis_at), (parts,), jnp.float32, smallest / len(cuts), top_value / len(cuts)))
        factor_of = factor_of * jnp.repeat(draws, dims[axis_at] // parts).reshape([-1 if axis == axis_at else 1 for axis in range(len(dims))])
    return factor_of


def noise(stream_key, shape, deviation, bound, cuts=(), kind=jnp.bfloat16):
    level = level_of(stream_key, shape, cuts, -0.22, 0.18) if cuts else 1.0
    array = jax.random.normal(stream_key, shape, jnp.float32) * deviation * level
    return jnp.minimum(jnp.maximum(array, -bound), bound).astype(kind)


def heavy_noise(own_key, shape, scale, bound, pieces, heavy, held_as=jnp.bfloat16):
    entries = scale * jax.random.normal(own_key, shape, jnp.float32)
    if pieces:
        entries = entries * level_of(own_key, shape, pieces, -0.22, 0.18)
    return jnp.clip(with_spikes(entries, jax.random.fold_in(own_key, 3), *heavy), -bound, bound).astype(held_as)


def setup_inputs(seed: int = 0) -> dict:
    key_of = jax.random.split(jax.random.key(seed), 6)
    hidden_acts = noise(key_of[0], (TOKENS, FF), 1.0, 6.0, ((0, 64), (1, 16)))
    out_grads = noise(key_of[1], (TOKENS, D), 1.0, 6.0, ((0, 1024),))
    seq_of_token = draw_seq_of_token(jax.random.fold_in(key_of[5], 71), 0)
    proj_in = heavy_noise(key_of[3], (FF, K_IN), FF ** -0.5, 0.046875, ((0, 16),), (0, 1, 16, 2.0))
    proj_out = noise(key_of[4], (D, K_OUT), (D * TOK_DEV // SEQ_DEV) ** -0.5, 0.0034179688)
    return dict(hidden_acts=hidden_acts, out_grads=out_grads, seq_of_token=seq_of_token, proj_in=proj_in, proj_out=proj_out)


def reference(hidden_acts, out_grads, seq_of_token, proj_in, proj_out):
    blocks_count = TOKENS // TOK_DEV
    acts_blocks = hidden_acts.reshape(blocks_count, TOK_DEV, FF)
    grads_blocks = out_grads.reshape(blocks_count, TOK_DEV, D)
    seg_blocks = seq_of_token.reshape(blocks_count, TOK_DEV)

    def one_block(inputs):
        acts_rows, grads_rows, seg_rows = inputs
        acts_low = jnp.dot(acts_rows, proj_in, preferred_element_type=jnp.float32)
        grads_low = jnp.dot(grads_rows, proj_out, preferred_element_type=jnp.float32)
        labels = jnp.arange(SEQ_DEV, dtype=jnp.int32)
        one_hot = (seg_rows[None, :] == labels[:, None]).astype(jnp.float32)
        weighted = one_hot[:, :, None] * acts_low[None, :, :]
        return jnp.einsum("stk,tj->skj", weighted, grads_low, precision=lax.Precision.HIGHEST)

    result = lax.map(one_block, (acts_blocks, grads_blocks, seg_blocks))
    return result.reshape(SEQS, K_IN, K_OUT)
```

```python
import jax
import jax.numpy as jnp
from jax import lax
from jax.sharding import PartitionSpec as P

SEQ_DEV = 2


def shards(hidden_acts, out_grads, seq_of_token, proj_in, proj_out):
    grads_rows = jnp.dot(out_grads, proj_out, preferred_element_type=jnp.float32)
    grads_low = lax.all_gather(grads_rows, "tensor", axis=0, tiled=True)
    acts_part = jnp.dot(hidden_acts, proj_in, preferred_element_type=jnp.float32)
    labels = jnp.arange(SEQ_DEV, dtype=jnp.int32)
    one_hot = (seq_of_token[:, None] == labels[None, :]).astype(jnp.float32)
    weighted = (one_hot[:, :, None] * grads_low[:, None, :]).reshape(grads_low.shape[0], -1)
    part = jnp.einsum("tk,tj->kj", acts_part, weighted, precision=lax.Precision.HIGHEST)
    own = lax.psum_scatter(part, "tensor", scatter_dimension=0, tiled=True)
    return own.reshape(own.shape[0], SEQ_DEV, -1).transpose(1, 0, 2)


def solution(mesh):
    in_specs = (P("dp", "tensor"), P(("dp", "tensor"), None), P("dp"), P("tensor", None), P())
    out_specs = P("dp", "tensor", None)
    return jax.shard_map(shards, mesh=mesh, in_specs=in_specs, out_specs=out_specs, check_vma=False)
```

```python
import jax
import jax.numpy as jnp
from jax import lax
from jax.experimental import pallas as pl
from jax.experimental.pallas import tpu as pltpu
from jax.sharding import PartitionSpec as P

SEQ_DEV = 2
SIDE = 4
N = SIDE * SIDE
TOK = 768
OWN_TOK = TOK // N
FF_DEV = 1792
D = 8192
K_IN = 256
OWN_K = K_IN // N
K_OUT = 128
ROWS = SEQ_DEV * OWN_K
A_CHUNKS = 3
A_ROWS = TOK // A_CHUNKS
G_CHUNKS = 4
G_COLS = D // G_CHUNKS
OFFSETS = [(dy, dx) for dy in range(SIDE) for dx in range(SIDE)]
MESH = pl.DeviceIdType.MESH


def kernel(acts_hbm, grads_hbm, seq_ref, pin_hbm, pout_hbm, out_ref,
           acts_v, grads_v, pin_v, pout_v, g_all, g_split, m_hi, m_lo, part, recv,
           load_sem, g_send, g_recv, p_send, p_recv):
    me = lax.axis_index("tensor")
    y, x = lax.div(me, SIDE), lax.rem(me, SIDE)

    def peer(dy, dx):
        return lax.rem(y + dy, SIDE) * SIDE + lax.rem(x + dx, SIDE)

    g_loads, a_loads = [], []
    for c in range(G_CHUNKS):
        cols = pl.ds(c * G_COLS, G_COLS)
        g_loads.append((
            pltpu.make_async_copy(grads_hbm.at[:, cols], grads_v.at[:, cols], load_sem.at[2 * c]),
            pltpu.make_async_copy(pout_hbm.at[cols], pout_v.at[cols], load_sem.at[2 * c + 1])))
    for c in range(A_CHUNKS):
        rows = pl.ds(c * A_ROWS, A_ROWS)
        a_loads.append(pltpu.make_async_copy(
            acts_hbm.at[rows], acts_v.at[rows], load_sem.at[2 * G_CHUNKS + c]))
    pin_load = pltpu.make_async_copy(pin_hbm, pin_v, load_sem.at[2 * G_CHUNKS + A_CHUNKS])
    for pair in g_loads:
        for load in pair:
            load.start()
    pin_load.start()
    for load in a_loads:
        load.start()

    barrier = pltpu.get_barrier_semaphore()
    for dy, dx in OFFSETS[1:]:
        pl.semaphore_signal(barrier, inc=1, device_id={"tensor": peer(dy, dx)}, device_id_type=MESH)

    rows_low = jnp.zeros((OWN_TOK, K_OUT), jnp.float32)
    for c, pair in enumerate(g_loads):
        for load in pair:
            load.wait()
        cols = pl.ds(c * G_COLS, G_COLS)
        rows_low += jnp.dot(grads_v[:, cols], pout_v[cols, :], preferred_element_type=jnp.float32)

    def g_slot(index):
        return g_all.at[pl.ds(pl.multiple_of(index * OWN_TOK, 8), OWN_TOK)]

    g_slot(me)[...] = rows_low
    pl.semaphore_wait(barrier, N - 1)
    g_copies = []
    for d, (dy, dx) in enumerate(OFFSETS):
        if d:
            copy = pltpu.make_async_remote_copy(
                src_ref=g_slot(me), dst_ref=g_slot(me), send_sem=g_send.at[d], recv_sem=g_recv.at[d],
                device_id={"tensor": peer(dy, dx)}, device_id_type=MESH)
            copy.start()
            g_copies.append(copy)

    pin_load.wait()
    for c, load in enumerate(a_loads):
        load.wait()
        rows = pl.ds(c * A_ROWS, A_ROWS)
        low = jnp.dot(acts_v[rows, :], pin_v[...], preferred_element_type=jnp.float32).T
        seq = seq_ref[:, rows]
        hi = low.astype(jnp.bfloat16)
        lo = (low - hi.astype(jnp.float32)).astype(jnp.bfloat16)
        for split, value in ((m_hi, hi), (m_lo, lo)):
            wide = value.astype(jnp.float32)
            for s in range(SEQ_DEV):
                masked = jnp.where(seq == s, wide, 0.0).astype(jnp.bfloat16)
                split[:, s, :, rows] = masked.reshape(N, OWN_K, A_ROWS)

    for d, (dy, dx) in enumerate(OFFSETS):
        if d:
            source = lax.rem(y + SIDE - dy, SIDE) * SIDE + lax.rem(x + SIDE - dx, SIDE)
            pltpu.make_async_remote_copy(
                src_ref=g_slot(source), dst_ref=g_slot(source), send_sem=g_send.at[d], recv_sem=g_recv.at[d],
                device_id={"tensor": peer(dy, dx)}, device_id_type=MESH).wait_recv()
    g = g_all[...]
    g_hi = g.astype(jnp.bfloat16)
    g_split[:, :K_OUT] = g_hi
    g_split[:, K_OUT:] = (g - g_hi.astype(jnp.float32)).astype(jnp.bfloat16)

    p_copies = []
    for dy in (2, 1, 3, 0):
        first = lax.rem(y + dy, SIDE) * SIDE
        a_hi = m_hi[pl.ds(first, SIDE)].reshape(SIDE * ROWS, TOK)
        a_lo = m_lo[pl.ds(first, SIDE)].reshape(SIDE * ROWS, TOK)
        both = jnp.dot(a_hi, g_split[...], preferred_element_type=jnp.float32)
        value = both[:, :K_OUT] + both[:, K_OUT:] + jnp.dot(
            a_lo, g_split[:, :K_OUT], preferred_element_type=jnp.float32)
        part[pl.ds(first, SIDE)] = value.reshape(SIDE, ROWS, K_OUT)
        for dx in (2, 1, 3, 0):
            d = dy * SIDE + dx
            if d:
                copy = pltpu.make_async_remote_copy(
                    src_ref=part.at[peer(dy, dx)], dst_ref=recv.at[d], send_sem=p_send.at[d],
                    recv_sem=p_recv.at[d], device_id={"tensor": peer(dy, dx)}, device_id_type=MESH)
                copy.start()
                p_copies.append((d, copy))

    total = part[me]
    for d, copy in p_copies:
        copy.wait_recv()
        total += recv[d]
    out_ref[...] = total.reshape(SEQ_DEV, OWN_K, K_OUT)
    for copy in g_copies:
        copy.wait_send()
    for d, copy in p_copies:
        copy.wait_send()


def shards(hidden_acts, out_grads, seq_of_token, proj_in, proj_out):
    hbm = pl.BlockSpec(memory_space=pl.ANY)
    vmem = pl.BlockSpec(memory_space=pltpu.VMEM)
    bf16, f32 = jnp.bfloat16, jnp.float32
    return pl.pallas_call(
        kernel,
        out_shape=jax.ShapeDtypeStruct((SEQ_DEV, OWN_K, K_OUT), f32),
        in_specs=[hbm, hbm, vmem, hbm, hbm],
        out_specs=vmem,
        scratch_shapes=[
            pltpu.VMEM((TOK, FF_DEV), bf16),
            pltpu.VMEM((OWN_TOK, D), bf16),
            pltpu.VMEM((FF_DEV, K_IN), bf16),
            pltpu.VMEM((D, K_OUT), bf16),
            pltpu.VMEM((TOK, K_OUT), f32),
            pltpu.VMEM((TOK, 2 * K_OUT), bf16),
            pltpu.VMEM((N, SEQ_DEV, OWN_K, TOK), bf16),
            pltpu.VMEM((N, SEQ_DEV, OWN_K, TOK), bf16),
            pltpu.VMEM((N, ROWS, K_OUT), f32),
            pltpu.VMEM((N, ROWS, K_OUT), f32),
            pltpu.SemaphoreType.DMA((2 * G_CHUNKS + A_CHUNKS + 1,)),
            pltpu.SemaphoreType.DMA((N,)),
            pltpu.SemaphoreType.DMA((N,)),
            pltpu.SemaphoreType.DMA((N,)),
            pltpu.SemaphoreType.DMA((N,)),
        ],
        compiler_params=pltpu.CompilerParams(collective_id=0, has_side_effects=True),
    )(hidden_acts, out_grads, seq_of_token.reshape(1, TOK), proj_in, proj_out)


def solution(mesh):
    in_specs = (P("dp", "tensor"), P(("dp", "tensor"), None), P("dp"), P("tensor", None), P())
    out_specs = P("dp", "tensor", None)
    return jax.shard_map(shards, mesh=mesh, in_specs=in_specs, out_specs=out_specs, check_vma=False)
```

```python
import jax
import jax.numpy as jnp
from jax import lax
from jax.experimental import pallas as pl
from jax.experimental.pallas import tpu as pltpu
from jax.sharding import PartitionSpec as P

SEQ_DEV = 2
SIDE = 4
N = SIDE * SIDE
TOK = 768
OWN_TOK = TOK // N
FF_DEV = 1792
D = 8192
K_IN = 256
OWN_K = K_IN // N
K_OUT = 128
ROWS = SEQ_DEV * OWN_K
A_CHUNKS = 3
A_ROWS = TOK // A_CHUNKS
G_CHUNKS = 4
G_COLS = D // G_CHUNKS
OFFSETS = [(dy, dx) for dy in (2, 1, 3, 0) for dx in (2, 1, 3, 0)][:-1]
OFFSETS.sort(key=lambda o: -min(o[0], SIDE - o[0]) - min(o[1], SIDE - o[1]))
LATE_LOADS = 2
MESH = pl.DeviceIdType.MESH


def kernel(acts_hbm, grads_hbm, seq_ref, pin_hbm, pout_hbm, out_ref,
           acts_v, grads_v, pin_v, pout_v, g_split, m_hi, m_lo, part, recv,
           load_sem, g_send, g_recv, p_send, p_recv):
    me = lax.axis_index("tensor")
    y, x = lax.div(me, SIDE), lax.rem(me, SIDE)

    def peer(dy, dx):
        return lax.rem(y + dy, SIDE) * SIDE + lax.rem(x + dx, SIDE)

    barrier = pltpu.get_barrier_semaphore()
    for dy, dx in OFFSETS:
        pl.semaphore_signal(barrier, inc=1, device_id={"tensor": peer(dy, dx)}, device_id_type=MESH)

    g_loads, a_loads = [], []
    for c in range(G_CHUNKS):
        cols = pl.ds(c * G_COLS, G_COLS)
        g_loads.append((
            pltpu.make_async_copy(grads_hbm.at[:, cols], grads_v.at[:, cols], load_sem.at[2 * c]),
            pltpu.make_async_copy(pout_hbm.at[cols], pout_v.at[cols], load_sem.at[2 * c + 1])))
    for c in range(A_CHUNKS):
        rows = pl.ds(c * A_ROWS, A_ROWS)
        a_loads.append(pltpu.make_async_copy(
            acts_hbm.at[rows], acts_v.at[rows], load_sem.at[2 * G_CHUNKS + c]))
    pin_load = pltpu.make_async_copy(pin_hbm, pin_v, load_sem.at[2 * G_CHUNKS + A_CHUNKS])
    for pair in g_loads:
        for load in pair:
            load.start()
    rows_low = jnp.zeros((OWN_TOK, K_OUT), jnp.float32)
    for c, pair in enumerate(g_loads):
        for load in pair:
            load.wait()
        if c == LATE_LOADS:
            pin_load.start()
            for load in a_loads:
                load.start()
        cols = pl.ds(c * G_COLS, G_COLS)
        rows_low += jnp.dot(grads_v[:, cols], pout_v[cols, :], preferred_element_type=jnp.float32)

    def g_slot(index):
        return g_split.at[pl.ds(pl.multiple_of(index * OWN_TOK, 16), OWN_TOK)]

    rows_hi = rows_low.astype(jnp.bfloat16)
    g_slot(me)[:, :K_OUT] = rows_hi
    g_slot(me)[:, K_OUT:] = (rows_low - rows_hi.astype(jnp.float32)).astype(jnp.bfloat16)
    pl.semaphore_wait(barrier, N - 1)
    g_copies = []
    for dy, dx in OFFSETS:
        d = dy * SIDE + dx
        copy = pltpu.make_async_remote_copy(
            src_ref=g_slot(me), dst_ref=g_slot(me), send_sem=g_send.at[d], recv_sem=g_recv.at[d],
            device_id={"tensor": peer(dy, dx)}, device_id_type=MESH)
        copy.start()
        g_copies.append(copy)

    pin_load.wait()
    for c, load in enumerate(a_loads):
        load.wait()
        rows = pl.ds(c * A_ROWS, A_ROWS)
        low = jnp.dot(acts_v[rows, :], pin_v[...], preferred_element_type=jnp.float32).T
        seq = seq_ref[rows][None, :]
        hi = low.astype(jnp.bfloat16)
        lo = (low - hi.astype(jnp.float32)).astype(jnp.bfloat16)
        for split, value in ((m_hi, hi), (m_lo, lo)):
            wide = value.astype(jnp.float32)
            for s in range(SEQ_DEV):
                masked = jnp.where(seq == s, wide, 0.0).astype(jnp.bfloat16)
                split[:, s, :, rows] = masked.reshape(N, OWN_K, A_ROWS)

    for dy, dx in OFFSETS:
        d = dy * SIDE + dx
        source = lax.rem(y + SIDE - dy, SIDE) * SIDE + lax.rem(x + SIDE - dx, SIDE)
        pltpu.make_async_remote_copy(
            src_ref=g_slot(source), dst_ref=g_slot(source), send_sem=g_send.at[d], recv_sem=g_recv.at[d],
            device_id={"tensor": peer(dy, dx)}, device_id_type=MESH).wait_recv()

    p_copies = []
    for dy in (2, 1, 3, 0):
        first = lax.rem(y + dy, SIDE) * SIDE
        a_hi = m_hi[pl.ds(first, SIDE)].reshape(SIDE * ROWS, TOK)
        a_lo = m_lo[pl.ds(first, SIDE)].reshape(SIDE * ROWS, TOK)
        both = jnp.dot(a_hi, g_split[...], preferred_element_type=jnp.float32)
        value = both[:, :K_OUT] + both[:, K_OUT:] + jnp.dot(
            a_lo, g_split[:, :K_OUT], preferred_element_type=jnp.float32)
        part[pl.ds(first, SIDE)] = value.reshape(SIDE, ROWS, K_OUT)
        for dx in (2, 1, 3, 0):
            d = dy * SIDE + dx
            if d:
                copy = pltpu.make_async_remote_copy(
                    src_ref=part.at[peer(dy, dx)], dst_ref=recv.at[d], send_sem=p_send.at[d],
                    recv_sem=p_recv.at[d], device_id={"tensor": peer(dy, dx)}, device_id_type=MESH)
                copy.start()
                p_copies.append((d, copy))

    total = part[me]
    for d, copy in p_copies:
        copy.wait_recv()
        total += recv[d]
    out_ref[...] = total.reshape(SEQ_DEV, OWN_K, K_OUT)
    for copy in g_copies:
        copy.wait_send()
    for d, copy in p_copies:
        copy.wait_send()


def shards(hidden_acts, out_grads, seq_of_token, proj_in, proj_out):
    hbm = pl.BlockSpec(memory_space=pl.ANY)
    vmem = pl.BlockSpec(memory_space=pltpu.VMEM)
    bf16, f32 = jnp.bfloat16, jnp.float32
    return pl.pallas_call(
        kernel,
        out_shape=jax.ShapeDtypeStruct((SEQ_DEV, OWN_K, K_OUT), f32),
        in_specs=[hbm, hbm, vmem, hbm, hbm],
        out_specs=vmem,
        scratch_shapes=[
            pltpu.VMEM((TOK, FF_DEV), bf16),
            pltpu.VMEM((OWN_TOK, D), bf16),
            pltpu.VMEM((FF_DEV, K_IN), bf16),
            pltpu.VMEM((D, K_OUT), bf16),
            pltpu.VMEM((TOK, 2 * K_OUT), bf16),
            pltpu.VMEM((N, SEQ_DEV, OWN_K, TOK), bf16),
            pltpu.VMEM((N, SEQ_DEV, OWN_K, TOK), bf16),
            pltpu.VMEM((N, ROWS, K_OUT), f32),
            pltpu.VMEM((N, ROWS, K_OUT), f32),
            pltpu.SemaphoreType.DMA((2 * G_CHUNKS + A_CHUNKS + 1,)),
            pltpu.SemaphoreType.DMA((N,)),
            pltpu.SemaphoreType.DMA((N,)),
            pltpu.SemaphoreType.DMA((N,)),
            pltpu.SemaphoreType.DMA((N,)),
        ],
        compiler_params=pltpu.CompilerParams(collective_id=0, has_side_effects=True),
    )(hidden_acts, out_grads, seq_of_token, proj_in, proj_out)


def solution(mesh):
    in_specs = (P("dp", "tensor"), P(("dp", "tensor"), None), P("dp"), P("tensor", None), P())
    out_specs = P("dp", "tensor", None)
    return jax.shard_map(shards, mesh=mesh, in_specs=in_specs, out_specs=out_specs, check_vma=False)
```

```python
import jax
import jax.numpy as jnp
from jax import lax
from jax.experimental import pallas as pl
from jax.experimental.pallas import tpu as pltpu
from jax.sharding import PartitionSpec as P

SEQ_DEV = 2
SIDE = 4
N = SIDE * SIDE
TOK = 768
OWN_TOK = TOK // N
FF_DEV = 1792
D = 8192
K_IN = 256
OWN_K = K_IN // N
K_OUT = 128
ROWS = SEQ_DEV * OWN_K
A_CHUNKS = 3
A_ROWS = TOK // A_CHUNKS
G_CHUNKS = 4
G_COLS = D // G_CHUNKS
OFFSETS = [(dy, dx) for dy in (2, 1, 3, 0) for dx in (2, 1, 3, 0)][:-1]
OFFSETS.sort(key=lambda o: -min(o[0], SIDE - o[0]) - min(o[1], SIDE - o[1]))
LATE_LOADS = 2
MESH = pl.DeviceIdType.MESH


def kernel(acts_hbm, grads_hbm, seq_hbm, pin_hbm, pout_hbm, out_ref,
           seq_ref, acts_v, grads_v, pin_v, pout_v, g_split, m_hi, m_lo, part, recv,
           load_sem, g_send, g_recv, p_send, p_recv):
    me = lax.axis_index("tensor")
    y, x = lax.div(me, SIDE), lax.rem(me, SIDE)

    def peer(dy, dx):
        return lax.rem(y + dy, SIDE) * SIDE + lax.rem(x + dx, SIDE)

    barrier = pltpu.get_barrier_semaphore()
    for dy, dx in OFFSETS:
        pl.semaphore_signal(barrier, inc=1, device_id={"tensor": peer(dy, dx)}, device_id_type=MESH)

    g_loads, a_loads = [], []
    for c in range(G_CHUNKS):
        cols = pl.ds(c * G_COLS, G_COLS)
        g_loads.append((
            pltpu.make_async_copy(grads_hbm.at[:, cols], grads_v.at[:, cols], load_sem.at[2 * c]),
            pltpu.make_async_copy(pout_hbm.at[cols], pout_v.at[cols], load_sem.at[2 * c + 1])))
    for c in range(A_CHUNKS):
        rows = pl.ds(c * A_ROWS, A_ROWS)
        a_loads.append(pltpu.make_async_copy(
            acts_hbm.at[rows], acts_v.at[rows], load_sem.at[2 * G_CHUNKS + c]))
    pin_load = pltpu.make_async_copy(pin_hbm, pin_v, load_sem.at[2 * G_CHUNKS + A_CHUNKS])
    seq_load = pltpu.make_async_copy(seq_hbm, seq_ref, load_sem.at[2 * G_CHUNKS + A_CHUNKS + 1])
    for pair in g_loads:
        for load in pair:
            load.start()
    rows_low = jnp.zeros((OWN_TOK, K_OUT), jnp.float32)
    for c, pair in enumerate(g_loads):
        for load in pair:
            load.wait()
        if c == LATE_LOADS:
            seq_load.start()
            pin_load.start()
            for load in a_loads:
                load.start()
        cols = pl.ds(c * G_COLS, G_COLS)
        rows_low += jnp.dot(grads_v[:, cols], pout_v[cols, :], preferred_element_type=jnp.float32)

    def g_slot(index):
        return g_split.at[pl.ds(pl.multiple_of(index * OWN_TOK, 16), OWN_TOK)]

    rows_hi = rows_low.astype(jnp.bfloat16)
    g_slot(me)[:, :K_OUT] = rows_hi
    g_slot(me)[:, K_OUT:] = (rows_low - rows_hi.astype(jnp.float32)).astype(jnp.bfloat16)
    pl.semaphore_wait(barrier, N - 1)
    g_copies = []
    for dy, dx in OFFSETS:
        d = dy * SIDE + dx
        copy = pltpu.make_async_remote_copy(
            src_ref=g_slot(me), dst_ref=g_slot(me), send_sem=g_send.at[d], recv_sem=g_recv.at[d],
            device_id={"tensor": peer(dy, dx)}, device_id_type=MESH)
        copy.start()
        g_copies.append(copy)

    seq_load.wait()
    pin_load.wait()
    for c, load in enumerate(a_loads):
        load.wait()
        rows = pl.ds(c * A_ROWS, A_ROWS)
        low = jnp.dot(acts_v[rows, :], pin_v[...], preferred_element_type=jnp.float32).T
        seq = seq_ref[rows][None, :]
        hi = low.astype(jnp.bfloat16)
        lo = (low - hi.astype(jnp.float32)).astype(jnp.bfloat16)
        for split, value in ((m_hi, hi), (m_lo, lo)):
            wide = value.astype(jnp.float32)
            for s in range(SEQ_DEV):
                masked = jnp.where(seq == s, wide, 0.0).astype(jnp.bfloat16)
                split[:, s, :, rows] = masked.reshape(N, OWN_K, A_ROWS)

    for dy, dx in OFFSETS:
        d = dy * SIDE + dx
        source = lax.rem(y + SIDE - dy, SIDE) * SIDE + lax.rem(x + SIDE - dx, SIDE)
        pltpu.make_async_remote_copy(
            src_ref=g_slot(source), dst_ref=g_slot(source), send_sem=g_send.at[d], recv_sem=g_recv.at[d],
            device_id={"tensor": peer(dy, dx)}, device_id_type=MESH).wait_recv()

    p_copies = []
    for dy in (2, 1, 3, 0):
        first = lax.rem(y + dy, SIDE) * SIDE
        a_hi = m_hi[pl.ds(first, SIDE)].reshape(SIDE * ROWS, TOK)
        a_lo = m_lo[pl.ds(first, SIDE)].reshape(SIDE * ROWS, TOK)
        both = jnp.dot(a_hi, g_split[...], preferred_element_type=jnp.float32)
        value = both[:, :K_OUT] + both[:, K_OUT:] + jnp.dot(
            a_lo, g_split[:, :K_OUT], preferred_element_type=jnp.float32)
        part[pl.ds(first, SIDE)] = value.reshape(SIDE, ROWS, K_OUT)
        for dx in (2, 1, 3, 0):
            d = dy * SIDE + dx
            if d:
                copy = pltpu.make_async_remote_copy(
                    src_ref=part.at[peer(dy, dx)], dst_ref=recv.at[d], send_sem=p_send.at[d],
                    recv_sem=p_recv.at[d], device_id={"tensor": peer(dy, dx)}, device_id_type=MESH)
                copy.start()
                p_copies.append((d, copy))

    total = part[me]
    for d, copy in p_copies:
        copy.wait_recv()
        total += recv[d]
    out_ref[...] = total.reshape(SEQ_DEV, OWN_K, K_OUT)
    for copy in g_copies:
        copy.wait_send()
    for d, copy in p_copies:
        copy.wait_send()


def shards(hidden_acts, out_grads, seq_of_token, proj_in, proj_out):
    hbm = pl.BlockSpec(memory_space=pl.ANY)
    vmem = pl.BlockSpec(memory_space=pltpu.VMEM)
    bf16, f32 = jnp.bfloat16, jnp.float32
    return pl.pallas_call(
        kernel,
        out_shape=pltpu.VMEM((SEQ_DEV, OWN_K, K_OUT), f32),
        in_specs=[hbm] * 5,
        out_specs=vmem,
        scratch_shapes=[
            pltpu.VMEM((TOK,), jnp.int32),
            pltpu.VMEM((TOK, FF_DEV), bf16),
            pltpu.VMEM((OWN_TOK, D), bf16),
            pltpu.VMEM((FF_DEV, K_IN), bf16),
            pltpu.VMEM((D, K_OUT), bf16),
            pltpu.VMEM((TOK, 2 * K_OUT), bf16),
            pltpu.VMEM((N, SEQ_DEV, OWN_K, TOK), bf16),
            pltpu.VMEM((N, SEQ_DEV, OWN_K, TOK), bf16),
            pltpu.VMEM((N, ROWS, K_OUT), f32),
            pltpu.VMEM((N, ROWS, K_OUT), f32),
            pltpu.SemaphoreType.DMA((2 * G_CHUNKS + A_CHUNKS + 2,)),
            pltpu.SemaphoreType.DMA((N,)),
            pltpu.SemaphoreType.DMA((N,)),
            pltpu.SemaphoreType.DMA((N,)),
            pltpu.SemaphoreType.DMA((N,)),
        ],
        compiler_params=pltpu.CompilerParams(collective_id=0, has_side_effects=True),
    )(hidden_acts, out_grads, seq_of_token, proj_in, proj_out)


def solution(mesh):
    in_specs = (P("dp", "tensor"), P(("dp", "tensor"), None), P("dp"), P("tensor", None), P())
    out_specs = P("dp", "tensor", None)
    return jax.shard_map(shards, mesh=mesh, in_specs=in_specs, out_specs=out_specs, check_vma=False)
```

```python
import jax
import jax.numpy as jnp
from jax import lax
from jax.experimental import pallas as pl
from jax.experimental.pallas import tpu as pltpu
from jax.sharding import PartitionSpec as P

SEQ_DEV = 2
SIDE = 4
N = SIDE * SIDE
TOK = 768
OWN_TOK = TOK // N
FF_DEV = 1792
D = 8192
K_IN = 256
OWN_K = K_IN // N
K_OUT = 128
ROWS = SEQ_DEV * OWN_K
A_CHUNKS = 3
A_ROWS = TOK // A_CHUNKS
G_CHUNKS = 8
G_COLS = D // G_CHUNKS
OFFSETS = [(dy, dx) for dy in (2, 1, 3, 0) for dx in (2, 1, 3, 0)][:-1]
OFFSETS.sort(key=lambda o: -min(o[0], SIDE - o[0]) - min(o[1], SIDE - o[1]))
LATE_LOADS = 5
MESH = pl.DeviceIdType.MESH


def kernel(acts_hbm, grads_hbm, seq_hbm, pin_hbm, pout_hbm, out_ref,
           seq_ref, acts_v, grads_v, pin_v, pout_v, g_split, m_hi, m_lo, part, recv,
           load_sem, g_send, g_recv, p_send, p_recv):
    me = lax.axis_index("tensor")
    y, x = lax.div(me, SIDE), lax.rem(me, SIDE)

    def peer(dy, dx):
        return lax.rem(y + dy, SIDE) * SIDE + lax.rem(x + dx, SIDE)

    barrier = pltpu.get_barrier_semaphore()
    for dy, dx in OFFSETS:
        pl.semaphore_signal(barrier, inc=1, device_id={"tensor": peer(dy, dx)}, device_id_type=MESH)

    g_loads, a_loads = [], []
    for c in range(G_CHUNKS):
        cols = pl.ds(c * G_COLS, G_COLS)
        g_loads.append((
            pltpu.make_async_copy(grads_hbm.at[:, cols], grads_v.at[:, cols], load_sem.at[2 * c]),
            pltpu.make_async_copy(pout_hbm.at[cols], pout_v.at[cols], load_sem.at[2 * c + 1])))
    for c in range(A_CHUNKS):
        rows = pl.ds(c * A_ROWS, A_ROWS)
        a_loads.append(pltpu.make_async_copy(
            acts_hbm.at[rows], acts_v.at[rows], load_sem.at[2 * G_CHUNKS + c]))
    pin_load = pltpu.make_async_copy(pin_hbm, pin_v, load_sem.at[2 * G_CHUNKS + A_CHUNKS])
    seq_load = pltpu.make_async_copy(seq_hbm, seq_ref, load_sem.at[2 * G_CHUNKS + A_CHUNKS + 1])
    for pair in g_loads:
        for load in pair:
            load.start()
    rows_low = jnp.zeros((OWN_TOK, K_OUT), jnp.float32)
    for c, pair in enumerate(g_loads):
        for load in pair:
            load.wait()
        if c == LATE_LOADS:
            seq_load.start()
            pin_load.start()
            for load in a_loads:
                load.start()
        cols = pl.ds(c * G_COLS, G_COLS)
        rows_low += jnp.dot(grads_v[:, cols], pout_v[cols, :], preferred_element_type=jnp.float32)

    def g_slot(index):
        return g_split.at[pl.ds(pl.multiple_of(index * OWN_TOK, 16), OWN_TOK)]

    rows_hi = rows_low.astype(jnp.bfloat16)
    g_slot(me)[:, :K_OUT] = rows_hi
    g_slot(me)[:, K_OUT:] = (rows_low - rows_hi.astype(jnp.float32)).astype(jnp.bfloat16)
    pl.semaphore_wait(barrier, N - 1)
    g_copies = []
    for dy, dx in OFFSETS:
        d = dy * SIDE + dx
        copy = pltpu.make_async_remote_copy(
            src_ref=g_slot(me), dst_ref=g_slot(me), send_sem=g_send.at[d], recv_sem=g_recv.at[d],
            device_id={"tensor": peer(dy, dx)}, device_id_type=MESH)
        copy.start()
        g_copies.append(copy)

    seq_load.wait()
    pin_load.wait()
    for c, load in enumerate(a_loads):
        load.wait()
        rows = pl.ds(c * A_ROWS, A_ROWS)
        low = jnp.dot(acts_v[rows, :], pin_v[...], preferred_element_type=jnp.float32).T
        seq = seq_ref[rows][None, :]
        hi = low.astype(jnp.bfloat16)
        lo = (low - hi.astype(jnp.float32)).astype(jnp.bfloat16)
        for split, value in ((m_hi, hi), (m_lo, lo)):
            wide = value.astype(jnp.float32)
            for s in range(SEQ_DEV):
                masked = jnp.where(seq == s, wide, 0.0).astype(jnp.bfloat16)
                split[:, s, :, rows] = masked.reshape(N, OWN_K, A_ROWS)

    for dy, dx in OFFSETS:
        d = dy * SIDE + dx
        source = lax.rem(y + SIDE - dy, SIDE) * SIDE + lax.rem(x + SIDE - dx, SIDE)
        pltpu.make_async_remote_copy(
            src_ref=g_slot(source), dst_ref=g_slot(source), send_sem=g_send.at[d], recv_sem=g_recv.at[d],
            device_id={"tensor": peer(dy, dx)}, device_id_type=MESH).wait_recv()

    p_copies = []
    for dy in (2, 1, 3, 0):
        first = lax.rem(y + dy, SIDE) * SIDE
        a_hi = m_hi[pl.ds(first, SIDE)].reshape(SIDE * ROWS, TOK)
        a_lo = m_lo[pl.ds(first, SIDE)].reshape(SIDE * ROWS, TOK)
        both = jnp.dot(a_hi, g_split[...], preferred_element_type=jnp.float32)
        value = both[:, :K_OUT] + both[:, K_OUT:] + jnp.dot(
            a_lo, g_split[:, :K_OUT], preferred_element_type=jnp.float32)
        part[pl.ds(first, SIDE)] = value.reshape(SIDE, ROWS, K_OUT)
        for dx in (2, 1, 3, 0):
            d = dy * SIDE + dx
            if d:
                copy = pltpu.make_async_remote_copy(
                    src_ref=part.at[peer(dy, dx)], dst_ref=recv.at[d], send_sem=p_send.at[d],
                    recv_sem=p_recv.at[d], device_id={"tensor": peer(dy, dx)}, device_id_type=MESH)
                copy.start()
                p_copies.append((d, copy))

    total = part[me]
    for d, copy in sorted(p_copies, key=lambda item: -OFFSETS.index((item[0] // SIDE, item[0] % SIDE))):
        copy.wait_recv()
        total += recv[d]
    out_ref[...] = total.reshape(SEQ_DEV, OWN_K, K_OUT)
    for copy in g_copies:
        copy.wait_send()
    for d, copy in p_copies:
        copy.wait_send()


def shards(hidden_acts, out_grads, seq_of_token, proj_in, proj_out):
    hbm = pl.BlockSpec(memory_space=pl.ANY)
    vmem = pl.BlockSpec(memory_space=pltpu.VMEM)
    bf16, f32 = jnp.bfloat16, jnp.float32
    return pl.pallas_call(
        kernel,
        out_shape=pltpu.VMEM((SEQ_DEV, OWN_K, K_OUT), f32),
        in_specs=[hbm] * 5,
        out_specs=vmem,
        scratch_shapes=[
            pltpu.VMEM((TOK,), jnp.int32),
            pltpu.VMEM((TOK, FF_DEV), bf16),
            pltpu.VMEM((OWN_TOK, D), bf16),
            pltpu.VMEM((FF_DEV, K_IN), bf16),
            pltpu.VMEM((D, K_OUT), bf16),
            pltpu.VMEM((TOK, 2 * K_OUT), bf16),
            pltpu.VMEM((N, SEQ_DEV, OWN_K, TOK), bf16),
            pltpu.VMEM((N, SEQ_DEV, OWN_K, TOK), bf16),
            pltpu.VMEM((N, ROWS, K_OUT), f32),
            pltpu.VMEM((N, ROWS, K_OUT), f32),
            pltpu.SemaphoreType.DMA((2 * G_CHUNKS + A_CHUNKS + 2,)),
            pltpu.SemaphoreType.DMA((N,)),
            pltpu.SemaphoreType.DMA((N,)),
            pltpu.SemaphoreType.DMA((N,)),
            pltpu.SemaphoreType.DMA((N,)),
        ],
        compiler_params=pltpu.CompilerParams(collective_id=0, has_side_effects=True),
    )(hidden_acts, out_grads, seq_of_token, proj_in, proj_out)


def solution(mesh):
    in_specs = (P("dp", "tensor"), P(("dp", "tensor"), None), P("dp"), P("tensor", None), P())
    out_specs = P("dp", "tensor", None)
    return jax.shard_map(shards, mesh=mesh, in_specs=in_specs, out_specs=out_specs, check_vma=False)
```
